32 devices in a mesh: wide: 8 (over z, y), narrow: 4 (over x, core).
Axes of the slice: x: 2, y: 2, z: 4, core: 2. Of those that a mesh axis runs over, the one named last changes fastest.
Arguments:
- inputs: bfloat16 [32, 192, 2048], P(('wide', 'narrow')), may hold values from -6 to 6
- counts: int32 [32], P(('wide', 'narrow')), may hold values from 0 to 48, as said below
- gain_attn: bfloat16 [2048], P(('wide', 'narrow')), may hold values from 0.5 to 1.5
- w_query: bfloat16 [2048, 2048], P(('wide', 'narrow')), may hold values from -0.125 to 0.125
- w_key: bfloat16 [2048, 2048], P(('wide', 'narrow')), may hold values from -0.125 to 0.125
- w_value: bfloat16 [2048, 2048], P(('wide', 'narrow')), may hold values from -0.125 to 0.125
- w_out: bfloat16 [2048, 2048], P(('wide', 'narrow')), may hold values from -0.5 to 0.5
- gain_mlp: bfloat16 [2048], P(('wide', 'narrow')), may hold values from 0.5 to 1.5
- w_up: bfloat16 [2048, 8192], P(('wide', 'narrow')), may hold values from -0.125 to 0.125
- w_down: bfloat16 [8192, 2048], P(('wide', 'narrow')), may hold values from -0.0625 to 0.0625
- cotangent: bfloat16 [32, 192, 2048], P(('wide', 'narrow')), may hold values from -6 to 6
Outputs:
- output: bfloat16 [32, 192, 2048], P(('wide', 'narrow'))
- grad_input: float32 [32, 192, 2048], P(('wide', 'narrow'))
- grad_gain_attn: float32 [2048], P(('wide', 'narrow'))
- grad_w_query: float32 [2048, 2048], P(('wide', 'narrow'))
- grad_w_key: float32 [2048, 2048], P(('wide', 'narrow'))
- grad_w_value: float32 [2048, 2048], P(('wide', 'narrow'))
- grad_w_out: float32 [2048, 2048], P(('wide', 'narrow'))
- grad_gain_mlp: float32 [2048], P(('wide', 'narrow'))
- grad_w_up: float32 [2048, 8192], P(('wide', 'narrow'))
- grad_w_down: float32 [8192, 2048], P(('wide', 'narrow'))
The draws below stay inside these ranges and needn't reach their ends.
Inputs may be any that keep to these rules, and one draw needn't show every extreme that they name: Item i holds 144 image tokens followed by counts[i] text and action tokens; its slots from 144 + counts[i] to 191 are padding. Some item has 48 such tokens and some has none.
All inputs are finite; a program needn't handle non-finite values.
Results may differ from the reference program's by a relative error of at most 0.013.
Values may be sent and summed in bfloat16 or wider, within the bound.
No kernel may reach another device: no remote copies, remote signals or barrier semaphores. Data moves between devices by JAX's collectives and lax.ppermute only.
A program may use at most 512 MiB of HBM per device.

```python
import math
import jax
import jax.numpy as jnp
from jax import lax

D = 2048
H = 16
HD = 128
FF = 8192
IMAGE = 144
TEXT_MAX = 48
SLOT = 192
ITEMS = 32


def draw_counts(key, part):
    key_values = jax.random.fold_in(key, 11)
    key_ranking = jax.random.fold_in(key, 23)
    values = jax.random.randint(key_values, (ITEMS,), 0, TEXT_MAX + 1)
    ranking = jax.random.permutation(key_ranking, ITEMS)
    values = values.at[ranking[0]].set(TEXT_MAX)
    values = values.at[ranking[1]].set(0)
    return values.astype(jnp.int32)


def with_spikes(entries, stream_key, source, target, blocks, factor):
    def block_of(axis_at):
        return (jnp.arange(entries.shape[axis_at]) // (entries.shape[axis_at] // blocks)).reshape((-1,) + (1,) * (entries.ndim - 1 - axis_at))

    first = jax.random.permutation(stream_key, blocks)[block_of(target)]
    second = (block_of(target) + blocks // 2) % blocks
    return jnp.where((block_of(source) == first) | (block_of(source) == second), factor * entries, entries)


def block_levels(own_key, extent, split, least, top_value):
    def one(dim, shards_of):
        steps = jax.random.uniform(jax.random.fold_in(jax.random.fold_in(own_key, 6), dim), (shards_of,), jnp.float32, least / len(split), top_value / len(split))
        return jnp.repeat(jnp.exp(steps), extent[dim] // shards_of).reshape((-1,) + (1,) * (len(extent) - dim - 1))

    level = one(*split[0])
    for cut in split[1:]:
        level = level * one(*cut)
    return level


def noise(stream_key, extent, deviation, bound, cuts=(), held_as=jnp.bfloat16):
    entries = deviation * jax.random.normal(stream_key, extent, jnp.float32)
    if cuts:
        entries = entries * block_levels(stream_key, extent, cuts, -0.22, 0.18)
    return jnp.clip(entries, -bound, bound).astype(held_as)


def heavy_noise(own_key, extent, deviation, limit, split, heavy, dtype=jnp.bfloat16):
    entries = deviation * jax.random.normal(own_key, extent, jnp.float32)
    if split:
        entries = entries * block_levels(own_key, extent, split, -0.22, 0.18)
    return jnp.clip(with_spikes(entries, jax.random.fold_in(own_key, 3), *heavy), -limit, limit).astype(dtype)


def setup_inputs(seed: int = 0) -> dict:
    seeds = jax.random.split(jax.random.key(seed), 12)
    inputs = heavy_noise(seeds[0], (ITEMS, SLOT, D), 1.0, 6.0, ((0, 32),), (0, 2, 32, 2.75))
    counts = draw_counts(jax.random.fold_in(seeds[11], 71), 0)
    gain_attn = jnp.clip(1.0 + 0.1 * jax.random.normal(seeds[2], (D,), jnp.float32), 0.5, 1.5).astype(jnp.bfloat16)
    w_query = noise(seeds[3], (D, D), D ** -0.5, 0.125, ((0, 32),))
    w_key = noise(seeds[4], (D, D), D ** -0.5, 0.125, ((0, 32),))
    w_value = noise(seeds[5], (D, D), D ** -0.5, 0.125, ((0, 32),))
    w_out = noise(seeds[6], (D, D), (D // 16) ** -0.5, 0.5, ((0, 32),))
    gain_mlp = jnp.clip(1.0 + 0.1 * jax.random.normal(seeds[7], (D,), jnp.float32), 0.5, 1.5).astype(jnp.bfloat16)
    w_up = noise(seeds[8], (D, FF), D ** -0.5, 0.125, ((0, 32),))
    w_down = noise(seeds[9], (FF, D), FF ** -0.5, 0.0625, ((0, 32),))
    cotangent = noise(seeds[10], (ITEMS, SLOT, D), 1.0, 6.0, ((0, 32),))
    return dict(inputs=inputs, counts=counts, gain_attn=gain_attn, w_query=w_query, w_key=w_key, w_value=w_value, w_out=w_out, gain_mlp=gain_mlp, w_up=w_up, w_down=w_down, cotangent=cotangent)


EPSILON = 1e-05
NEG_LARGE = -1e+30

@jax.custom_vjp
def low(v):
    return lax.optimization_barrier(v.astype(jnp.bfloat16)).astype(jnp.float32)

@jax.custom_vjp
def low_back(v):
    return v

def low_keep(v):
    return (low(v), None)

def low_pass(kept, grad):
    return (grad,)

def back_keep(v):
    return (v, None)

def back_low(kept, grad):
    return (low(grad),)
low.defvjp(low_keep, low_pass)
low_back.defvjp(back_keep, back_low)

def matmul(left_side, right_side):
    return jnp.dot(left_side, right_side, precision=lax.Precision.HIGHEST, preferred_element_type=jnp.float32)

def layer_norm(values, gain):
    center = values - lax.optimization_barrier(jnp.mean(values, axis=-1, keepdims=True))
    variance = lax.optimization_barrier(jnp.mean(center * center, axis=-1, keepdims=True))
    return center * lax.rsqrt(variance + EPSILON) * gain

def both_round(values):
    return low(low_back(values))

def group_forward(params, group_inputs, group_lengths):
    gain_attn, w_query, w_key, w_value, w_out, gain_mlp, w_up, w_down = params
    item_count = group_inputs.shape[0]
    row_values = group_inputs.reshape(item_count * SLOT, D)
    normed_a = low(layer_norm(row_values, gain_attn))
    queries = both_round(matmul(normed_a, w_query)).reshape(item_count, SLOT, H, HD)
    key_rows = both_round(matmul(normed_a, w_key)).reshape(item_count, SLOT, H, HD)
    value_rows = both_round(matmul(normed_a, w_value)).reshape(item_count, SLOT, H, HD)
    raw = jnp.einsum('ishd,ithd->ihst', queries, key_rows, precision=lax.Precision.HIGHEST)
    scores = low_back(raw * HD ** (-0.5))
    position = jnp.arange(SLOT)
    causal = (position[None, :] <= position[:, None])[None, None]
    live_keys = position[None, None, None, :] < group_lengths[:, None, None, None]
    masked = jnp.where(causal & live_keys, scores, NEG_LARGE)
    row_peak = lax.optimization_barrier(jnp.max(masked, axis=-1, keepdims=True))
    shifted = jnp.exp(masked - row_peak)
    attn_probs = low(shifted / lax.optimization_barrier(jnp.sum(shifted, axis=-1, keepdims=True)))
    mixed = jnp.einsum('ihst,ithd->ishd', attn_probs, value_rows, precision=lax.Precision.HIGHEST)
    mixed = both_round(mixed).reshape(item_count * SLOT, D)
    residual = row_values + low_back(matmul(mixed, w_out))
    normed_m = low(layer_norm(residual, gain_mlp))
    hidden = low_back(matmul(normed_m, w_up))
    active = low(jax.nn.gelu(hidden, approximate=True))
    result = residual + low_back(matmul(active, w_down))
    return result.reshape(item_count, SLOT, D)

def forward(inputs, counts, params):
    lengths = counts + IMAGE
    group_size = math.gcd(ITEMS, 16)
    grouped_inputs = inputs.reshape(ITEMS // group_size, group_size, SLOT, D)
    grouped_lengths = lengths.reshape(ITEMS // group_size, group_size)
    step_fn = jax.checkpoint(group_forward)
    results = lax.map(lambda pieces: step_fn(params, pieces[0], pieces[1]), (grouped_inputs, grouped_lengths))
    return results.reshape(ITEMS, SLOT, D)

def reference(inputs, counts, gain_attn, w_query, w_key, w_value, w_out, gain_mlp, w_up, w_down, cotangent):
    floats = tuple((item.astype(jnp.float32) for item in (gain_attn, w_query, w_key, w_value, w_out, gain_mlp, w_up, w_down)))
    stream = inputs.astype(jnp.float32)

    def closed(values, *params):
        return forward(values, counts, params)
    result, pullback = jax.vjp(closed, stream, *floats)
    lengths = counts + IMAGE
    valid_rows = (jnp.arange(SLOT)[None, :] < lengths[:, None]).astype(jnp.float32)
    grads = pullback(cotangent.astype(jnp.float32) * valid_rows[:, :, None])
    return (result.astype(jnp.bfloat16), grads[0], grads[1], grads[2], grads[3], grads[4], grads[5], grads[6], grads[7], grads[8])
```

```python
import jax
import jax.numpy as jnp
from jax import lax
from jax.sharding import Mesh, PartitionSpec as P

H = 16
HD = 128
IMAGE = 144
EPSILON = 1e-05
NEG_LARGE = -1e30

ALL = ("z", "y", "x", "c")
TEAM = ("y", "x", "c")
SWAP = [(0, 1), (1, 0)]


def matmul(left_side, right_side):
    return jnp.dot(left_side, right_side, preferred_element_type=jnp.float32)


def gram_rows(left_side, right_side):
    return lax.dot_general(
        left_side, right_side, (((0,), (0,)), ((), ())), preferred_element_type=jnp.float32
    )


def times_transposed(left_side, right_side):
    return lax.dot_general(
        left_side, right_side, (((1,), (1,)), ((), ())), preferred_element_type=jnp.float32
    )


def gelu_tanh(values):
    return jax.nn.gelu(values, approximate=True)


def norm_stats(values):
    center = values - jnp.mean(values, axis=-1, keepdims=True)
    inverse = lax.rsqrt(jnp.mean(center * center, axis=-1, keepdims=True) + EPSILON)
    return (center * inverse, inverse)


def norm_backward(grad_scaled, scaled, inverse):
    first_mean = jnp.mean(grad_scaled, axis=-1, keepdims=True)
    second_mean = jnp.mean(grad_scaled * scaled, axis=-1, keepdims=True)
    return inverse * (grad_scaled - first_mean - scaled * second_mean)


def swap(block, axis):
    return lax.ppermute(block, axis, SWAP)


def team_gather(block):
    half = block.shape[0] // 2
    by_x = swap(block, "x")
    by_y = swap(block, "y")
    by_c = swap(block, "c")
    corner = jnp.concatenate([swap(by_x[:half], "y"), swap(by_y[half:], "x")], axis=0)
    return jnp.concatenate(
        [block, by_c, by_x, swap(by_x, "c"), by_y, swap(by_y, "c"), corner, swap(corner, "c")], axis=0
    )


def team_sum(parts):
    low = jnp.bfloat16
    half = parts.shape[1] // 2

    def pair(k):
        return parts[k].astype(jnp.float32) + swap(parts[k + 1], "c").astype(jnp.float32)

    corner = pair(6).astype(low)
    on_x = pair(2)
    on_y = pair(4)
    from_x = swap(corner[:half], "x").astype(jnp.float32)
    from_y = swap(corner[half:], "y").astype(jnp.float32)
    x_first = swap(on_x[:half].astype(low), "x")
    y_last = swap(on_y[half:].astype(low), "y")
    own = pair(0)
    y_first = swap((on_y[:half] + from_x).astype(low), "y")
    x_last = swap((on_x[half:] + from_y).astype(low), "x")
    return (
        own
        + jnp.concatenate([x_first, x_last], axis=0).astype(jnp.float32)
        + jnp.concatenate([y_first, y_last], axis=0).astype(jnp.float32)
    )


def weight_gather(block):
    return lax.all_gather(block, "z", axis=0, tiled=True)


def weight_scatter(terms):
    return lax.psum_scatter(terms.astype(jnp.bfloat16), "z", scatter_dimension=0, tiled=True)


def masked_scores(queries, key_rows, allowed, score_scale):
    raw = jnp.einsum("ishd,ithd->ihst", queries, key_rows, preferred_element_type=jnp.float32)
    return jnp.where(allowed, raw * score_scale, NEG_LARGE)


def per_device(
    inputs, counts, gain_attn, w_query, w_key, w_value, w_out, gain_mlp, w_up, w_down, cotangent
):
    low = jnp.bfloat16
    layers = lax.axis_size("z")
    team = lax.axis_size(TEAM)
    devices = layers * team
    item_count, slot_count, features = inputs.shape
    assert item_count == 1
    row_count = item_count * slot_count
    wide_rows = row_count * team
    depth = w_query.shape[0]
    head_parts = HD // depth
    head_axes = TEAM[len(TEAM) - (head_parts.bit_length() - 1) :]
    head_groups = team // head_parts
    own_heads = layers // head_parts
    own_width = own_heads * HD
    units = w_down.shape[0]
    own_units = layers * units
    score_scale = HD ** (-0.5)

    def own_columns(weight):
        cut = weight.reshape(depth, head_parts, own_heads, head_groups, HD)
        return cut.transpose(3, 1, 0, 2, 4).reshape(team, depth, own_width)

    qkv_cut = jnp.concatenate([own_columns(w_query), own_columns(w_key), own_columns(w_value)], axis=2)
    qkv_cut = lax.all_to_all(qkv_cut, TEAM, 0, 0, tiled=True)
    w_qkv = weight_gather(qkv_cut.reshape(team * depth, 3 * own_width))
    out_rows = weight_gather(w_out)

    small = jnp.stack(
        [gain_attn, gain_mlp, jnp.broadcast_to(counts.astype(low)[:1], gain_attn.shape)], axis=0
    )
    small = lax.all_to_all(
        jnp.broadcast_to(small[None], (devices,) + small.shape), ALL, 0, 0, tiled=True
    )
    full_gain_a = small[:, 0].reshape(1, features).astype(jnp.float32)
    full_gain_m = small[:, 1].reshape(1, features).astype(jnp.float32)
    member = lax.axis_index("z") * team + (lax.axis_index(TEAM) ^ jnp.arange(team))
    picked = member[:, None] == jnp.arange(devices)[None, :]
    team_counts = jnp.sum(jnp.where(picked, small[:, 2, 0].astype(jnp.float32)[None, :], 0.0), axis=1)

    stream = inputs.reshape(row_count, features).astype(jnp.float32)
    scaled_a, inverse_a = norm_stats(stream)
    normed_a = team_gather((scaled_a * full_gain_a).astype(low))

    up_cut = w_up.reshape(depth, layers, team, units).transpose(2, 0, 1, 3)
    up_cut = lax.all_to_all(up_cut.reshape(team, depth, own_units), TEAM, 0, 0, tiled=True)
    w_up_own = weight_gather(up_cut.reshape(team * depth, own_units))
    w_down_own = weight_gather(w_down)

    position = jnp.arange(slot_count)
    lengths = counts + IMAGE
    live = (position[None, :] < lengths[:, None]).reshape(row_count, 1)
    cotangent_low = jnp.where(live, cotangent.reshape(row_count, features), jnp.zeros((), low))
    grad_stream = cotangent_low.astype(jnp.float32)
    grad_low = team_gather(cotangent_low)

    out_cut = out_rows.reshape(head_parts, own_heads, depth, features)
    out_cut = lax.all_to_all(out_cut, head_axes, 0, 0, tiled=True)
    w_out_own = out_cut.transpose(1, 0, 2, 3).reshape(own_width, features)

    qkv = matmul(normed_a, w_qkv).astype(low)
    head_shape = (team, slot_count, own_heads, HD)
    queries = qkv[:, :own_width].reshape(head_shape)
    key_rows = qkv[:, own_width : 2 * own_width].reshape(head_shape)
    value_rows = qkv[:, 2 * own_width :].reshape(head_shape)
    causal = (position[None, :] <= position[:, None])[None, None]
    live_keys = position[None, :].astype(jnp.float32) < team_counts[:, None] + float(IMAGE)
    allowed = causal & live_keys[:, None, None, :]
    masked = masked_scores(queries, key_rows, allowed, score_scale)
    row_peak = jnp.max(masked, axis=-1, keepdims=True)
    shifted = jnp.exp(masked - row_peak)
    attn_probs = shifted / jnp.sum(shifted, axis=-1, keepdims=True)
    probs_low = attn_probs.astype(low)
    mixed = jnp.einsum("ihst,ithd->ishd", probs_low, value_rows, preferred_element_type=jnp.float32)
    mixed = mixed.astype(low).reshape(wide_rows, own_width)
    out_terms = matmul(mixed, w_out_own).astype(low)
    residual = stream + team_sum(out_terms.reshape(team, row_count, features))

    scaled_m, inverse_m = norm_stats(residual)
    normed_m = team_gather((scaled_m * full_gain_m).astype(low))
    hidden = matmul(normed_m, w_up_own)
    gelu_value, gelu_back = jax.vjp(gelu_tanh, hidden)
    active = gelu_value.astype(low)
    down_terms = matmul(active, w_down_own).astype(low)
    output = residual + team_sum(down_terms.reshape(team, row_count, features))

    grad_active = times_transposed(grad_low, w_down_own)
    grad_hidden = gelu_back(grad_active)[0].astype(low)
    normed_m_terms = times_transposed(grad_hidden, w_up_own).astype(low)
    grad_normed_m = team_sum(normed_m_terms.reshape(team, row_count, features))
    grad_down = weight_scatter(gram_rows(active, grad_low))
    grad_up = weight_scatter(gram_rows(normed_m, grad_hidden))
    gain_m_terms = jnp.sum(grad_normed_m * scaled_m, axis=0)
    grad_residual = norm_backward(grad_normed_m * full_gain_m, scaled_m, inverse_m) + grad_stream

    grad_residual_low = team_gather(grad_residual.astype(low))
    grad_out = gram_rows(mixed, grad_residual_low).astype(low)
    grad_out = grad_out.reshape(own_heads, head_parts, depth, features).transpose(1, 0, 2, 3)
    grad_out = lax.all_to_all(grad_out, head_axes, 0, 0, tiled=True)
    grad_out = weight_scatter(grad_out.reshape(layers * depth, features))
    grad_mixed = times_transposed(grad_residual_low, w_out_own).astype(low).reshape(head_shape)
    grad_values = jnp.einsum(
        "ihst,ishd->ithd", probs_low, grad_mixed, preferred_element_type=jnp.float32
    ).astype(low)
    grad_probs = jnp.einsum(
        "ishd,ithd->ihst", grad_mixed, value_rows, preferred_element_type=jnp.float32
    )
    row_delta = jnp.sum(attn_probs * grad_probs, axis=-1, keepdims=True)
    grad_scores = (attn_probs * (grad_probs - row_delta)).astype(low)
    grad_queries = (
        jnp.einsum("ihst,ithd->ishd", grad_scores, key_rows, preferred_element_type=jnp.float32)
        * score_scale
    ).astype(low)
    grad_keys = (
        jnp.einsum("ihst,ishd->ithd", grad_scores, queries, preferred_element_type=jnp.float32)
        * score_scale
    ).astype(low)
    grad_qkv = jnp.concatenate(
        [part.reshape(wide_rows, own_width) for part in (grad_queries, grad_keys, grad_values)], axis=1
    )
    normed_a_terms = times_transposed(grad_qkv, w_qkv).astype(low)
    grad_qkv_w = weight_scatter(gram_rows(normed_a, grad_qkv))
    grad_normed_a = team_sum(normed_a_terms.reshape(team, row_count, features))
    gain_a_terms = jnp.sum(grad_normed_a * scaled_a, axis=0)
    grad_input = norm_backward(grad_normed_a * full_gain_a, scaled_a, inverse_a) + grad_residual

    gain_terms = jnp.stack([gain_a_terms, gain_m_terms], axis=0).reshape(2, devices, depth)
    gain_terms = lax.all_to_all(gain_terms.transpose(1, 0, 2), ALL, 0, 0, tiled=True)
    gain_grads = jnp.sum(gain_terms, axis=0)

    def all_columns(cut):
        cut = cut.reshape(head_groups, head_parts, depth, own_heads, HD)
        return cut.transpose(2, 1, 3, 0, 4).reshape(depth, features).astype(jnp.float32)

    grad_up = lax.all_to_all(grad_up.reshape(team, depth, own_units), TEAM, 0, 0, tiled=True)
    grad_up = grad_up.reshape(team, depth, layers, units).transpose(1, 2, 0, 3)
    grad_up = grad_up.reshape(depth, layers * team * units).astype(jnp.float32)
    back = lax.all_to_all(grad_qkv_w.reshape(team, depth, 3 * own_width), TEAM, 0, 0, tiled=True)

    return (
        output.reshape(item_count, slot_count, features).astype(low),
        grad_input.reshape(item_count, slot_count, features),
        gain_grads[0],
        all_columns(back[:, :, :own_width]),
        all_columns(back[:, :, own_width : 2 * own_width]),
        all_columns(back[:, :, 2 * own_width :]),
        grad_out.astype(jnp.float32),
        gain_grads[1],
        grad_up,
        grad_down.astype(jnp.float32),
    )


def solution(mesh):
    wide, narrow = mesh.shape["wide"], mesh.shape["narrow"]
    steps = Mesh(mesh.devices.reshape(wide // 2, 2, narrow // 2, 2), ALL)
    rows, items = P(ALL, None), P(ALL, None, None)
    return jax.shard_map(
        per_device,
        mesh=steps,
        in_specs=(items, P(ALL), P(ALL), rows, rows, rows, rows, P(ALL), rows, rows, items),
        out_specs=(items, items, P(ALL), rows, rows, rows, rows, P(ALL), rows, rows),
        check_vma=False,
    )
```

```python
import jax
import jax.numpy as jnp
from jax import lax
from jax.experimental import pallas as pl
from jax.experimental.pallas import tpu as pltpu
from jax.sharding import Mesh, PartitionSpec as P

H = 16
HD = 128
IMAGE = 144
EPSILON = 1e-05
NEG_LARGE = -1e30

ALL = ("z", "y", "x", "c")
TEAM = ("y", "x", "c")
SWAP = [(0, 1), (1, 0)]


def matmul(left_side, right_side):
    return jnp.dot(left_side, right_side, preferred_element_type=jnp.float32)


def gram_rows(left_side, right_side):
    return lax.dot_general(
        left_side, right_side, (((0,), (0,)), ((), ())), preferred_element_type=jnp.float32
    )


def times_transposed(left_side, right_side):
    return lax.dot_general(
        left_side, right_side, (((1,), (1,)), ((), ())), preferred_element_type=jnp.float32
    )


def gelu_tanh(values):
    return jax.nn.gelu(values, approximate=True)


def norm_stats(values):
    center = values - jnp.mean(values, axis=-1, keepdims=True)
    inverse = lax.rsqrt(jnp.mean(center * center, axis=-1, keepdims=True) + EPSILON)
    return (center * inverse, inverse)


def norm_backward(grad_scaled, scaled, inverse):
    first_mean = jnp.mean(grad_scaled, axis=-1, keepdims=True)
    second_mean = jnp.mean(grad_scaled * scaled, axis=-1, keepdims=True)
    return inverse * (grad_scaled - first_mean - scaled * second_mean)


FIRST = (2, 4)
SECOND = (4, 2)
ORDER = ((0, 2, 4, 6, 1, 5, 3, 7), (0, 4, 2, 6, 1, 3, 5, 7))


def first_hop(block):
    return lax.ppermute(block, TEAM, [(t, t ^ FIRST[t & 1]) for t in range(8)])


def second_hop(block):
    return lax.ppermute(block, TEAM, [(t, t ^ SECOND[t & 1]) for t in range(8)])


def core_hop(block):
    return lax.ppermute(block, TEAM, [(t, t ^ 1) for t in range(8)])


def after(value, *others):
    return lax.optimization_barrier((value, *others))[0]


def team_gather(block, *others):
    near = first_hop(block)
    if others:
        near = after(near, *others)
    pair = jnp.concatenate([block, near], axis=0)
    other = second_hop(pair)
    return jnp.concatenate([pair, other, core_hop(pair), core_hop(other)], axis=0)


def team_sum(terms_of, rows, held=None, beside=None):
    low = jnp.bfloat16
    half = rows.shape[0] // 2
    quarter = half // 2
    arrived = core_hop(terms_of(rows[half:]).astype(low))
    near = terms_of(rows[:half]) + arrived.astype(jnp.float32)
    if beside is not None:
        held = after(held, arrived)
    far = second_hop(near[quarter:].astype(low))
    near = near[:quarter] + far.astype(jnp.float32)
    last = first_hop(near[quarter // 2 :].astype(low))
    if beside is None:
        return near[: quarter // 2] + last.astype(jnp.float32)
    result = beside(held)
    last, result = lax.optimization_barrier((last, result))
    return near[: quarter // 2] + last.astype(jnp.float32), result


def meet(kept, sent):
    arrived = core_hop(sent)
    core = lax.axis_index("c")
    return jnp.stack([jnp.where(core == 0, kept, arrived), jnp.where(core == 0, arrived, kept)], axis=1)


def own_part(parts):
    core = lax.axis_index("c")
    return jnp.where(core == 0, parts[0], parts[1]), jnp.where(core == 0, parts[1], parts[0])


def weight_gather(block):
    return lax.all_gather(block, "z", axis=0, tiled=True)


def weight_scatter(terms):
    return lax.psum_scatter(terms.astype(jnp.bfloat16), "z", scatter_dimension=0, tiled=True)


def probs_of(item_lengths, qkv, head, width):
    slots = qkv.shape[0]
    queries = qkv[:, head * HD : (head + 1) * HD]
    key_rows = qkv[:, width + head * HD : width + (head + 1) * HD]
    value_rows = qkv[:, 2 * width + head * HD : 2 * width + (head + 1) * HD]
    row = lax.broadcasted_iota(jnp.int32, (slots, slots), 0)
    col = lax.broadcasted_iota(jnp.int32, (slots, slots), 1)
    allowed = (col <= row) & (col < item_lengths[pl.program_id(0)])
    masked = jnp.where(allowed, times_transposed(queries, key_rows) * HD ** (-0.5), NEG_LARGE)
    shifted = jnp.exp(masked - jnp.max(masked, axis=-1, keepdims=True))
    return queries, key_rows, value_rows, shifted / jnp.sum(shifted, axis=-1, keepdims=True)


def attend_kernel(item_lengths, qkv, mixed):
    width = mixed.shape[1]
    for head in range(width // HD):
        _, _, value_rows, probs = probs_of(item_lengths, qkv, head, width)
        own = matmul(probs.astype(mixed.dtype), value_rows)
        mixed[:, head * HD : (head + 1) * HD] = own.astype(mixed.dtype)


def attend_back_kernel(item_lengths, qkv, grad_mixed, grad_qkv):
    width = grad_mixed.shape[1]
    low = grad_qkv.dtype
    score_scale = HD ** (-0.5)
    for head in range(width // HD):
        queries, key_rows, value_rows, probs = probs_of(item_lengths, qkv, head, width)
        grad_own = grad_mixed[:, head * HD : (head + 1) * HD]
        grad_probs = times_transposed(grad_own, value_rows)
        row_delta = jnp.sum(probs * grad_probs, axis=-1, keepdims=True)
        grad_scores = (probs * (grad_probs - row_delta)).astype(low)
        at = head * HD
        grad_qkv[:, at : at + HD] = (matmul(grad_scores, key_rows) * score_scale).astype(low)
        at += width
        grad_qkv[:, at : at + HD] = (gram_rows(grad_scores, queries) * score_scale).astype(low)
        at += width
        grad_qkv[:, at : at + HD] = gram_rows(probs.astype(low), grad_own).astype(low)


def attend_call(kernel, name, slots, lengths, operands, width, products):
    rows = operands[0].shape[0]
    own = operands[-1].shape[1] if products > 2 else width
    size = 2 * rows * slots * HD * products * (own // HD)

    def spec(columns):
        return pl.BlockSpec((slots, columns), lambda item, _: (item, 0))

    return pl.pallas_call(
        kernel,
        out_shape=jax.ShapeDtypeStruct((rows, width), operands[0].dtype),
        grid_spec=pltpu.PrefetchScalarGridSpec(
            num_scalar_prefetch=1,
            grid=(rows // slots,),
            in_specs=[spec(operand.shape[1]) for operand in operands],
            out_specs=spec(width),
        ),
        cost_estimate=pl.CostEstimate(
            flops=size,
            bytes_accessed=2 * rows * (width + sum(operand.shape[1] for operand in operands)),
            transcendentals=rows * slots * (own // HD),
        ),
        name=name,
    )(lengths, *operands)


def per_device(
    inputs, counts, gain_attn, w_query, w_key, w_value, w_out, gain_mlp, w_up, w_down, cotangent
):
    low = jnp.bfloat16
    layers = lax.axis_size("z")
    team = lax.axis_size(TEAM)
    devices = layers * team
    item_count, slot_count, features = inputs.shape
    assert item_count == 1
    row_count = item_count * slot_count
    wide_rows = row_count * team
    depth = w_query.shape[0]
    head_parts = HD // depth
    head_axes = TEAM[len(TEAM) - (head_parts.bit_length() - 1) :]
    head_groups = team // head_parts
    own_heads = layers // head_parts
    own_width = own_heads * HD
    units = w_down.shape[0]
    own_units = layers * units

    def own_columns(weight):
        cut = weight.reshape(depth, head_parts, own_heads, head_groups, HD)
        return cut.transpose(3, 1, 0, 2, 4).reshape(team, depth, own_width)

    qkv_cut = jnp.concatenate([own_columns(w_query), own_columns(w_key), own_columns(w_value)], axis=2)
    qkv_cut = lax.all_to_all(qkv_cut, TEAM, 0, 0, tiled=True).reshape(team * depth, 3 * own_width)
    strip = features // team
    out_cut = w_out.reshape(depth, team, strip).transpose(1, 0, 2).reshape(team * depth, strip)
    w_attn = weight_gather(jnp.concatenate([qkv_cut, out_cut], axis=1))
    up_cut = w_up.reshape(depth, layers, team, units).transpose(2, 0, 1, 3)
    up_cut = lax.all_to_all(up_cut.reshape(team, depth, own_units), TEAM, 0, 0, tiled=True)
    up_cut = up_cut.reshape(team * depth, own_units)
    strips = features // own_units
    down_cut = w_down.reshape(units, strips, own_units).transpose(1, 0, 2)
    down_cut = down_cut.reshape(team * depth, own_units)
    w_mlp = weight_gather(jnp.concatenate([up_cut, down_cut], axis=1))

    small = jnp.stack(
        [gain_attn, gain_mlp, jnp.broadcast_to(counts.astype(low)[:1], gain_attn.shape)], axis=0
    )
    small = lax.all_to_all(
        jnp.broadcast_to(small[None], (devices,) + small.shape), ALL, 0, 0, tiled=True
    )
    full_gain_a = small[:, 0].reshape(1, features).astype(jnp.float32)
    full_gain_m = small[:, 1].reshape(1, features).astype(jnp.float32)
    member = lax.axis_index("z") * team + (lax.axis_index(TEAM) ^ jnp.array(ORDER)[lax.axis_index("c")])
    picked = member[:, None] == jnp.arange(devices)[None, :]
    team_counts = jnp.sum(jnp.where(picked, small[:, 2, 0].astype(jnp.float32)[None, :], 0.0), axis=1)
    team_lengths = team_counts.astype(jnp.int32) + IMAGE

    stream = inputs.reshape(row_count, features).astype(jnp.float32)
    scaled_a, inverse_a = norm_stats(stream)
    normed_a = team_gather((scaled_a * full_gain_a).astype(low))

    position = jnp.arange(slot_count)
    lengths = counts + IMAGE
    live = (position[None, :] < lengths[:, None]).reshape(row_count, 1)
    cotangent_low = jnp.where(live, cotangent.reshape(row_count, features), jnp.zeros((), low))
    grad_stream = cotangent_low.astype(jnp.float32)
    grad_low = team_gather(cotangent_low)
    normed_a = after(normed_a, up_cut, grad_low)

    w_qkv = w_attn[:, : 3 * own_width]
    qkv = matmul(normed_a, w_qkv).astype(low)
    out_rows = w_attn[:, 3 * own_width :].reshape(layers, team, depth, strip)
    out_rows = out_rows.transpose(0, 2, 1, 3).reshape(layers, depth, features)
    if head_parts == 2:
        w_out_own = meet(*own_part(out_rows.reshape(2, own_heads, depth, features)))
    else:
        out_rows = out_rows.reshape(head_parts, own_heads, depth, features)
        w_out_own = lax.all_to_all(out_rows, head_axes, 0, 0, tiled=True).transpose(1, 0, 2, 3)
    w_out_own = w_out_own.reshape(own_width, features)
    mixed = attend_call(attend_kernel, "attend", slot_count, team_lengths, (qkv,), own_width, 2)
    residual = stream + team_sum(lambda rows: matmul(rows, w_out_own), mixed)

    scaled_m, inverse_m = norm_stats(residual)
    normed_m = team_gather((scaled_m * full_gain_m).astype(low))
    w_up_own = w_mlp[:, :own_units]
    w_down_own = w_mlp[:, own_units:].reshape(layers, strips, units, own_units)
    w_down_own = w_down_own.transpose(0, 2, 1, 3).reshape(own_units, features)
    hidden = matmul(normed_m, w_up_own)
    gelu_value, gelu_back = jax.vjp(gelu_tanh, hidden)
    active = gelu_value.astype(low)

    grad_down = gram_rows(active, grad_low).astype(low)
    grad_down, grad_low = lax.optimization_barrier((grad_down, grad_low))
    grad_down = weight_scatter(grad_down)
    grad_active = times_transposed(grad_low, w_down_own)
    grad_hidden = gelu_back(grad_active)[0].astype(low)
    grad_normed_m, grad_up = team_sum(
        lambda rows: times_transposed(rows, w_up_own),
        grad_hidden,
        grad_hidden,
        lambda held: gram_rows(normed_m, held).astype(low),
    )
    grad_up = weight_scatter(grad_up)
    gain_m_terms = jnp.sum(grad_normed_m * scaled_m, axis=0)
    grad_residual = norm_backward(grad_normed_m * full_gain_m, scaled_m, inverse_m) + grad_stream

    grad_residual_low = team_gather(grad_residual.astype(low))
    grad_mixed = times_transposed(grad_residual_low, w_out_own).astype(low)
    grad_qkv = attend_call(
        attend_back_kernel, "attend_back", slot_count, team_lengths, (qkv, grad_mixed), 3 * own_width, 6
    )
    grad_out = gram_rows(mixed, grad_residual_low).astype(low)
    grad_out = grad_out.reshape(own_heads, head_parts, depth, features).transpose(1, 0, 2, 3)
    if head_parts == 2:
        kept, sent = own_part(grad_out)
        arrived = core_hop(sent)
        core = lax.axis_index("c")
        grad_out = jnp.concatenate(
            [jnp.where(core == 0, kept, arrived), jnp.where(core == 0, arrived, kept)], axis=0
        )
    else:
        grad_out = lax.all_to_all(grad_out, head_axes, 0, 0, tiled=True)
    grad_out = grad_out.reshape(layers, depth, team, strip).transpose(0, 2, 1, 3)
    grad_out = grad_out.reshape(features, strip)
    grad_qkv_w = gram_rows(normed_a, grad_qkv).astype(low)
    grad_attn = weight_scatter(jnp.concatenate([grad_qkv_w, grad_out], axis=1))
    grad_qkv_w = grad_attn[:, : 3 * own_width]
    grad_out = grad_attn[:, 3 * own_width :].reshape(team, depth, strip)
    grad_out = grad_out.transpose(1, 0, 2).reshape(depth, features)
    grad_normed_a = team_sum(lambda rows: times_transposed(rows, w_qkv), grad_qkv)
    active = after(active, grad_qkv)
    output = residual + team_sum(lambda rows: matmul(rows, w_down_own), active)
    gain_a_terms = jnp.sum(grad_normed_a * scaled_a, axis=0)
    grad_input = norm_backward(grad_normed_a * full_gain_a, scaled_a, inverse_a) + grad_residual

    gain_terms = jnp.stack([gain_a_terms, gain_m_terms], axis=0).reshape(2, devices, depth)
    gain_terms = lax.all_to_all(gain_terms.transpose(1, 0, 2), ALL, 0, 0, tiled=True)
    gain_grads = jnp.sum(gain_terms, axis=0)

    def all_columns(cut):
        cut = cut.reshape(head_groups, head_parts, depth, own_heads, HD)
        return cut.transpose(2, 1, 3, 0, 4).reshape(depth, features).astype(jnp.float32)

    grad_up = lax.all_to_all(grad_up.reshape(team, depth, own_units), TEAM, 0, 0, tiled=True)
    grad_up = grad_up.reshape(team, depth, layers, units).transpose(1, 2, 0, 3)
    grad_up = grad_up.reshape(depth, layers * team * units).astype(jnp.float32)
    back = lax.all_to_all(grad_qkv_w.reshape(team, depth, 3 * own_width), TEAM, 0, 0, tiled=True)

    return (
        output.reshape(item_count, slot_count, features).astype(low),
        grad_input.reshape(item_count, slot_count, features),
        gain_grads[0],
        all_columns(back[:, :, :own_width]),
        all_columns(back[:, :, own_width : 2 * own_width]),
        all_columns(back[:, :, 2 * own_width :]),
        grad_out.astype(jnp.float32),
        gain_grads[1],
        grad_up,
        grad_down.astype(jnp.float32),
    )


def solution(mesh):
    wide, narrow = mesh.shape["wide"], mesh.shape["narrow"]
    steps = Mesh(mesh.devices.reshape(wide // 2, 2, narrow // 2, 2), ALL)
    rows, items = P(ALL, None), P(ALL, None, None)
    return jax.shard_map(
        per_device,
        mesh=steps,
        in_specs=(items, P(ALL), P(ALL), rows, rows, rows, rows, P(ALL), rows, rows, items),
        out_specs=(items, items, P(ALL), rows, rows, rows, rows, P(ALL), rows, rows),
        check_vma=False,
    )
```

```python
import math

import jax
import jax.numpy as jnp
from jax import lax
from jax.experimental import pallas as pl
from jax.experimental.pallas import tpu as pltpu
from jax.sharding import Mesh, PartitionSpec as P

H = 16
HD = 128
IMAGE = 144
EPSILON = 1e-05
NEG_LARGE = -1e30

ALL = ("z", "y", "x", "c")
TEAM = ("y", "x", "c")
SWAP = [(0, 1), (1, 0)]


def matmul(left_side, right_side):
    return jnp.dot(left_side, right_side, preferred_element_type=jnp.float32)


def gram_rows(left_side, right_side):
    return lax.dot_general(
        left_side, right_side, (((0,), (0,)), ((), ())), preferred_element_type=jnp.float32
    )


def times_transposed(left_side, right_side):
    return lax.dot_general(
        left_side, right_side, (((1,), (1,)), ((), ())), preferred_element_type=jnp.float32
    )


def gelu_tanh(values):
    inner = (2.0 / math.pi) ** 0.5 * (values + 0.044715 * values * values * values)
    return 0.5 * values * (1.0 + jnp.tanh(inner))


def norm_stats(values):
    center = values - jnp.mean(values, axis=-1, keepdims=True)
    inverse = lax.rsqrt(jnp.mean(center * center, axis=-1, keepdims=True) + EPSILON)
    return (center * inverse, inverse)


def norm_backward(grad_scaled, scaled, inverse):
    first_mean = jnp.mean(grad_scaled, axis=-1, keepdims=True)
    second_mean = jnp.mean(grad_scaled * scaled, axis=-1, keepdims=True)
    return inverse * (grad_scaled - first_mean - scaled * second_mean)


FIRST = (2, 4)
SECOND = (4, 2)
ORDER = ((0, 2, 4, 6, 1, 5, 3, 7), (0, 4, 2, 6, 1, 3, 5, 7))


def first_hop(block):
    return lax.ppermute(block, TEAM, [(t, t ^ FIRST[t & 1]) for t in range(8)])


def second_hop(block):
    return lax.ppermute(block, TEAM, [(t, t ^ SECOND[t & 1]) for t in range(8)])


def core_hop(block):
    return lax.ppermute(block, TEAM, [(t, t ^ 1) for t in range(8)])


def after(value, *others):
    return lax.optimization_barrier((value, *others))[0]


def team_gather(block, *others):
    near = first_hop(block)
    if others:
        near = after(near, *others)
    pair = jnp.concatenate([block, near], axis=0)
    other = second_hop(pair)
    return pair, other, core_hop(pair), core_hop(other)


def join(blocks):
    return jnp.concatenate(blocks, axis=0)


def team_sum(terms_of, rows, held=None):
    low = jnp.bfloat16
    half = rows.shape[0] // 2
    quarter = half // 2
    arrived = core_hop(terms_of(rows[half:]).astype(low))
    near = terms_of(rows[:half]) + arrived.astype(jnp.float32)
    far = second_hop(near[quarter:].astype(low))
    near = near[:quarter] + far.astype(jnp.float32)
    last = first_hop(near[quarter // 2 :].astype(low))
    total = near[: quarter // 2] + last.astype(jnp.float32)
    return total if held is None else (total, after(held, arrived))


def meet(kept, sent):
    arrived = core_hop(sent)
    core = lax.axis_index("c")
    return jnp.stack([jnp.where(core == 0, kept, arrived), jnp.where(core == 0, arrived, kept)], axis=1)


def own_part(parts):
    core = lax.axis_index("c")
    return jnp.where(core == 0, parts[0], parts[1]), jnp.where(core == 0, parts[1], parts[0])


def weight_gather(block):
    return lax.all_gather(block, "z", axis=0, tiled=True)


def weight_scatter(terms):
    return lax.psum_scatter(terms.astype(jnp.bfloat16), "z", scatter_dimension=0, tiled=True)


def probs_of(item_lengths, qkv, head, width):
    slots = qkv.shape[0]
    queries = qkv[:, head * HD : (head + 1) * HD]
    key_rows = qkv[:, width + head * HD : width + (head + 1) * HD]
    value_rows = qkv[:, 2 * width + head * HD : 2 * width + (head + 1) * HD]
    row = lax.broadcasted_iota(jnp.int32, (slots, slots), 0)
    col = lax.broadcasted_iota(jnp.int32, (slots, slots), 1)
    allowed = (col <= row) & (col < item_lengths[pl.program_id(0)])
    masked = jnp.where(allowed, times_transposed(queries, key_rows) * HD ** (-0.5), NEG_LARGE)
    shifted = jnp.exp(masked - jnp.max(masked, axis=-1, keepdims=True))
    return queries, key_rows, value_rows, shifted / jnp.sum(shifted, axis=-1, keepdims=True)


def attend_kernel(item_lengths, qkv, mixed):
    width = mixed.shape[1]
    for head in range(width // HD):
        _, _, value_rows, probs = probs_of(item_lengths, qkv, head, width)
        own = matmul(probs.astype(mixed.dtype), value_rows)
        mixed[:, head * HD : (head + 1) * HD] = own.astype(mixed.dtype)


def attend_back_kernel(item_lengths, qkv, grad_mixed, grad_qkv):
    width = grad_mixed.shape[1]
    low = grad_qkv.dtype
    score_scale = HD ** (-0.5)
    for head in range(width // HD):
        queries, key_rows, value_rows, probs = probs_of(item_lengths, qkv, head, width)
        grad_own = grad_mixed[:, head * HD : (head + 1) * HD]
        grad_probs = times_transposed(grad_own, value_rows)
        row_delta = jnp.sum(probs * grad_probs, axis=-1, keepdims=True)
        grad_scores = (probs * (grad_probs - row_delta)).astype(low)
        at = head * HD
        grad_qkv[:, at : at + HD] = (matmul(grad_scores, key_rows) * score_scale).astype(low)
        at += width
        grad_qkv[:, at : at + HD] = (gram_rows(grad_scores, queries) * score_scale).astype(low)
        at += width
        grad_qkv[:, at : at + HD] = gram_rows(probs.astype(low), grad_own).astype(low)


def mlp_kernel(*refs):
    *parts, grad_low, w_up, w_down, active, grad_hidden, terms, normed = refs
    step = pl.program_id(0)
    blocks, strips, units, columns = w_down.shape
    width = w_up.shape[3]
    low = active.dtype

    @pl.when(step == 0)
    def _():
        rows = parts[0].shape[0]
        for at, part in enumerate(parts):
            normed[at * rows : (at + 1) * rows] = part[...]

    hidden = matmul(normed[...], w_up[...].reshape(-1, width))
    value, back = jax.vjp(gelu_tanh, hidden)
    own = value.astype(low)
    active[...] = own
    grad_active = 0.0
    for s in range(strips):
        part = w_down[:, s].reshape(width, columns)
        grad_active += times_transposed(grad_low[:, s * columns : (s + 1) * columns], part)
    own_grad = back(grad_active)[0].astype(low)
    grad_hidden[...] = own_grad
    for s in range(strips):
        part = gram_rows(own, grad_low[:, s * columns : (s + 1) * columns]).astype(low)
        terms[pl.ds(step * blocks, blocks), s, :, columns:] = part.reshape(blocks, units, columns)
    part = gram_rows(normed[...], own_grad).astype(low)
    at = pl.multiple_of(step * width, width)
    terms[:, :, :, pl.ds(at, width)] = part.reshape(terms.shape[:3] + (width,))


def mlp_call(parts, grad_low, weights):
    rows, features = grad_low.shape
    layers, strips, units, columns = weights.shape
    own_units = columns // 2
    blocks = max(1, 256 // units)
    width = blocks * units
    low = grad_low.dtype

    def whole(shape):
        return pl.BlockSpec(shape, lambda step: (0,) * len(shape), pipeline_mode=pl.Buffered(1))

    return pl.pallas_call(
        mlp_kernel,
        out_shape=(
            jax.ShapeDtypeStruct((rows, own_units), low),
            jax.ShapeDtypeStruct((rows, own_units), low),
            jax.ShapeDtypeStruct(weights.shape, low),
        ),
        grid=(own_units // width,),
        in_specs=[whole(part.shape) for part in parts]
        + [
            whole((rows, features)),
            pl.BlockSpec((layers, strips, units, width), lambda step: (0, 0, 0, step)),
            pl.BlockSpec((blocks, strips, units, own_units), lambda step: (step, 0, 0, 1)),
        ],
        out_specs=(
            pl.BlockSpec((rows, width), lambda step: (0, step)),
            pl.BlockSpec((rows, width), lambda step: (0, step)),
            whole(weights.shape),
        ),
        scratch_shapes=[pltpu.VMEM((rows, features), low)],
        cost_estimate=pl.CostEstimate(
            flops=8 * rows * features * own_units,
            bytes_accessed=4 * rows * (features + own_units) + 8 * features * own_units,
            transcendentals=rows * own_units,
        ),
        name="mlp",
    )(*parts, grad_low, weights, weights)


def attend_call(kernel, name, slots, lengths, operands, width, products):
    rows = operands[0].shape[0]
    own = operands[-1].shape[1] if products > 2 else width
    size = 2 * rows * slots * HD * products * (own // HD)

    def spec(columns):
        return pl.BlockSpec((slots, columns), lambda item, _: (item, 0))

    return pl.pallas_call(
        kernel,
        out_shape=jax.ShapeDtypeStruct((rows, width), operands[0].dtype),
        grid_spec=pltpu.PrefetchScalarGridSpec(
            num_scalar_prefetch=1,
            grid=(rows // slots,),
            in_specs=[spec(operand.shape[1]) for operand in operands],
            out_specs=spec(width),
        ),
        cost_estimate=pl.CostEstimate(
            flops=size,
            bytes_accessed=2 * rows * (width + sum(operand.shape[1] for operand in operands)),
            transcendentals=rows * slots * (own // HD),
        ),
        name=name,
    )(lengths, *operands)


def per_device(
    inputs, counts, gain_attn, w_query, w_key, w_value, w_out, gain_mlp, w_up, w_down, cotangent
):
    low = jnp.bfloat16
    layers = lax.axis_size("z")
    team = lax.axis_size(TEAM)
    devices = layers * team
    item_count, slot_count, features = inputs.shape
    assert item_count == 1
    row_count = item_count * slot_count
    wide_rows = row_count * team
    depth = w_query.shape[0]
    head_parts = HD // depth
    head_axes = TEAM[len(TEAM) - (head_parts.bit_length() - 1) :]
    head_groups = team // head_parts
    own_heads = layers // head_parts
    own_width = own_heads * HD
    units = w_down.shape[0]
    own_units = layers * units

    def own_columns(weight):
        cut = weight.reshape(depth, head_parts, own_heads, head_groups, HD)
        return cut.transpose(3, 1, 0, 2, 4).reshape(team, depth, own_width)

    qkv_cut = jnp.concatenate([own_columns(w_query), own_columns(w_key), own_columns(w_value)], axis=2)
    qkv_cut = lax.all_to_all(qkv_cut, TEAM, 0, 0, tiled=True).reshape(team * depth, 3 * own_width)
    out_rows = weight_gather(w_out)
    w_qkv = weight_gather(qkv_cut)
    up_cut = w_up.reshape(depth, layers, team, units).transpose(2, 0, 1, 3)
    up_cut = lax.all_to_all(up_cut.reshape(team, depth, own_units), TEAM, 0, 0, tiled=True)
    up_cut = up_cut.reshape(team * depth, own_units)
    strips = features // own_units
    down_cut = w_down.reshape(units, strips, own_units).transpose(1, 0, 2)
    down_cut = down_cut.reshape(team * depth, own_units)
    w_mlp = weight_gather(jnp.concatenate([up_cut, down_cut], axis=1))

    small = jnp.stack(
        [gain_attn, gain_mlp, jnp.broadcast_to(counts.astype(low)[:1], gain_attn.shape)], axis=0
    )
    small = lax.all_to_all(
        jnp.broadcast_to(small[None], (devices,) + small.shape), ALL, 0, 0, tiled=True
    )
    full_gain_a = small[:, 0].reshape(1, features).astype(jnp.float32)
    full_gain_m = small[:, 1].reshape(1, features).astype(jnp.float32)
    member = lax.axis_index("z") * team + (lax.axis_index(TEAM) ^ jnp.array(ORDER)[lax.axis_index("c")])
    picked = member[:, None] == jnp.arange(devices)[None, :]
    team_counts = jnp.sum(jnp.where(picked, small[:, 2, 0].astype(jnp.float32)[None, :], 0.0), axis=1)
    team_lengths = team_counts.astype(jnp.int32) + IMAGE

    stream = inputs.reshape(row_count, features).astype(jnp.float32)
    scaled_a, inverse_a = norm_stats(stream)
    normed_a = team_gather((scaled_a * full_gain_a).astype(low))

    position = jnp.arange(slot_count)
    lengths = counts + IMAGE
    live = (position[None, :] < lengths[:, None]).reshape(row_count, 1)
    cotangent_low = jnp.where(live, cotangent.reshape(row_count, features), jnp.zeros((), low))
    grad_stream = cotangent_low.astype(jnp.float32)
    grad_low = team_gather(cotangent_low)
    normed_a = join(after(normed_a, up_cut, grad_low))
    grad_low = join(grad_low)

    qkv = matmul(normed_a, w_qkv).astype(low)
    out_rows = out_rows.reshape(layers, depth, features)
    if head_parts == 2:
        w_out_own = meet(*own_part(out_rows.reshape(2, own_heads, depth, features)))
    else:
        out_rows = out_rows.reshape(head_parts, own_heads, depth, features)
        w_out_own = lax.all_to_all(out_rows, head_axes, 0, 0, tiled=True).transpose(1, 0, 2, 3)
    w_out_own = w_out_own.reshape(own_width, features)
    mixed = attend_call(attend_kernel, "attend", slot_count, team_lengths, (qkv,), own_width, 2)
    residual = stream + team_sum(lambda rows: matmul(rows, w_out_own), mixed)

    scaled_m, inverse_m = norm_stats(residual)
    normed_m = team_gather((scaled_m * full_gain_m).astype(low))
    normed_m, w_mlp = lax.optimization_barrier((normed_m, w_mlp))
    w_up_own = w_mlp[:, :own_units]

    weights = w_mlp.reshape(layers, strips, units, 2 * own_units)
    active, grad_hidden, grad_mlp = mlp_call(normed_m, grad_low, weights)
    grad_mlp = weight_scatter(grad_mlp.reshape(features, 2 * own_units))
    w_down_own = jnp.concatenate(
        [weights[:, s, :, own_units:].reshape(own_units, own_units) for s in range(strips)], axis=1
    )
    w_down_own = lax.optimization_barrier(w_down_own)
    grad_normed_m = team_sum(lambda rows: times_transposed(rows, w_up_own), grad_hidden)
    gain_m_terms = jnp.sum(grad_normed_m * scaled_m, axis=0)
    grad_residual = norm_backward(grad_normed_m * full_gain_m, scaled_m, inverse_m) + grad_stream

    grad_residual_low = join(team_gather(grad_residual.astype(low)))
    grad_mixed = times_transposed(grad_residual_low, w_out_own).astype(low)
    grad_qkv = attend_call(
        attend_back_kernel, "attend_back", slot_count, team_lengths, (qkv, grad_mixed), 3 * own_width, 6
    )
    grad_out = gram_rows(mixed, grad_residual_low).astype(low)
    grad_out = grad_out.reshape(own_heads, head_parts, depth, features).transpose(1, 0, 2, 3)
    if head_parts == 2:
        kept, sent = own_part(grad_out)
        arrived = core_hop(sent)
        core = lax.axis_index("c")
        grad_out = jnp.concatenate(
            [jnp.where(core == 0, kept, arrived), jnp.where(core == 0, arrived, kept)], axis=0
        )
    else:
        grad_out = lax.all_to_all(grad_out, head_axes, 0, 0, tiled=True)
    strip = features // team
    grad_out = grad_out.reshape(layers, depth, team, strip).transpose(0, 2, 1, 3)
    grad_out = grad_out.reshape(features, strip)
    grad_qkv_w = gram_rows(normed_a, grad_qkv).astype(low)
    grad_attn = jnp.concatenate([grad_qkv_w, grad_out], axis=1)
    grad_qkv, grad_attn = lax.optimization_barrier((grad_qkv, grad_attn))
    grad_attn = weight_scatter(grad_attn)
    grad_qkv_w = grad_attn[:, : 3 * own_width]
    grad_out = grad_attn[:, 3 * own_width :].reshape(team, depth, strip)
    grad_out = grad_out.transpose(1, 0, 2).reshape(depth, features)
    grad_normed_a, active = team_sum(lambda rows: times_transposed(rows, w_qkv), grad_qkv, active)
    output = residual + team_sum(lambda rows: matmul(rows, w_down_own), active)
    gain_a_terms = jnp.sum(grad_normed_a * scaled_a, axis=0)
    grad_input = norm_backward(grad_normed_a * full_gain_a, scaled_a, inverse_a) + grad_residual

    gain_terms = jnp.stack([gain_a_terms, gain_m_terms], axis=0).reshape(2, devices, depth)
    gain_terms = lax.all_to_all(gain_terms.transpose(1, 0, 2), ALL, 0, 0, tiled=True)
    gain_grads = jnp.sum(gain_terms, axis=0)

    def all_columns(cut):
        cut = cut.reshape(head_groups, head_parts, depth, own_heads, HD)
        return cut.transpose(2, 1, 3, 0, 4).reshape(depth, features).astype(jnp.float32)

    grad_up = grad_mlp[:, :own_units]
    grad_down = jnp.concatenate(
        [grad_mlp[s * units : (s + 1) * units, own_units:] for s in range(strips)], axis=1
    )
    grad_up = lax.all_to_all(grad_up.reshape(team, depth, own_units), TEAM, 0, 0, tiled=True)
    grad_up = grad_up.reshape(team, depth, layers, units).transpose(1, 2, 0, 3)
    grad_up = grad_up.reshape(depth, layers * team * units).astype(jnp.float32)
    back = lax.all_to_all(grad_qkv_w.reshape(team, depth, 3 * own_width), TEAM, 0, 0, tiled=True)

    return (
        output.reshape(item_count, slot_count, features).astype(low),
        grad_input.reshape(item_count, slot_count, features),
        gain_grads[0],
        all_columns(back[:, :, :own_width]),
        all_columns(back[:, :, own_width : 2 * own_width]),
        all_columns(back[:, :, 2 * own_width :]),
        grad_out.astype(jnp.float32),
        gain_grads[1],
        grad_up,
        grad_down.astype(jnp.float32),
    )


def solution(mesh):
    wide, narrow = mesh.shape["wide"], mesh.shape["narrow"]
    steps = Mesh(mesh.devices.reshape(wide // 2, 2, narrow // 2, 2), ALL)
    rows, items = P(ALL, None), P(ALL, None, None)
    return jax.shard_map(
        per_device,
        mesh=steps,
        in_specs=(items, P(ALL), P(ALL), rows, rows, rows, rows, P(ALL), rows, rows, items),
        out_specs=(items, items, P(ALL), rows, rows, rows, rows, P(ALL), rows, rows),
        check_vma=False,
    )
```
